32 devices in a mesh: ra: 16 (over z, x, core), freq: 2 (over y).
Axes of the slice: x: 2, y: 2, z: 4, core: 2. Of those that a mesh axis runs over, the one named last changes fastest.
Arguments:
- solution: float32 [1920, 2048], P('freq', 'ra'), may hold values from -6 to 6
- residual: float32 [1920, 2048], P('freq', 'ra'), may hold values from -20 to 20
- direction: float32 [1920, 2048], P('freq', 'ra'), may hold values from -20 to 20
- sidereal: float32 [64], P('ra'), may hold values from -3.140625 to 3.140625
- response: float32 [64, 640], P('ra'), may hold values from 0.03 to 0.3
- significant: int32 [64, 10], P('ra'), may hold values from 0 to 1, as said below
- inv_noise: float32 [64, 1920], P('ra', 'freq'), may hold values from 0.25 to 4
Outputs:
- solution_next: float32 [1920, 2048], P('freq', 'ra')
- residual_next: float32 [1920, 2048], P('freq', 'ra')
- direction_next: float32 [1920, 2048], P('freq', 'ra')
The draws below stay inside these ranges and needn't reach their ends.
Inputs may be any that keep to these rules, and one draw needn't show every extreme that they name: `significant`: the ones of a row form one run of consecutive columns.
All inputs are finite; a program needn't handle non-finite values.
Results may differ from the reference program's by a relative error of at most 0.0003.
Values sent between devices are 32-bit elements; how exact they have to be, the bound alone decides.
A program may use at most 64 MiB of HBM per device.

```python
import math
import jax
import jax.numpy as jnp
from jax import lax

NDEC = 64
RA_DEV = 2
SEG_DEV = 4
PIX_DEV = 128
WINPIX = 640
WIN_TILES = 10
NF = 1920
NPIX = 2048
NSEG = 64
N_RA = 16


def rising_field(key):
    first, second, third = jax.random.split(key, 3)
    freq_pos = jnp.arange(NF, dtype=jnp.int32).astype(jnp.float32) / NF
    pixel_pos = jnp.arange(NPIX, dtype=jnp.int32).astype(jnp.float32) / NPIX
    row_rough = jax.random.uniform(first, (NF,), jnp.float32)
    col_rough = jax.random.uniform(second, (NPIX,), jnp.float32)
    spread = 10.0 ** ((row_rough[:, None] + col_rough[None, :]) / 2.0 - 0.5)
    product = (1.0 + 2.0 * freq_pos)[:, None] * (1.0 + 2.0 * pixel_pos)[None, :]
    trend = jnp.sqrt(product) / 3.0
    base = jnp.clip(jax.random.normal(third, (NF, NPIX), jnp.float32), -6.0, 6.0)
    return base * trend * spread


def draw_residual(key, part):
    return rising_field(jax.random.fold_in(key, 11))


def draw_direction(key, part):
    return rising_field(jax.random.fold_in(key, 23))


def draw_significant(key, part):
    first, second = jax.random.split(jax.random.fold_in(key, 37))
    offset = jax.random.randint(first, (NSEG, 1), -RA_DEV, RA_DEV + 1)
    half_width = jax.random.randint(second, (NSEG, 1), RA_DEV, 3 * RA_DEV + 1)
    columns = jnp.arange(WIN_TILES, dtype=jnp.int32)[None, :]
    distance = jnp.abs(2 * columns + 1 - 5 * RA_DEV - 2 * offset)
    return (distance < 2 * half_width).astype(jnp.int32)


def levels(key, dims, shards, smallest, high):
    def one(dim, shards_of):
        draws = jax.random.uniform(jax.random.fold_in(jax.random.fold_in(key, 6), dim), (shards_of,), jnp.float32, smallest / len(shards), high / len(shards))
        return jnp.repeat(jnp.exp(draws), dims[dim] // shards_of).reshape((-1,) + (1,) * (len(dims) - dim - 1))

    level = one(*shards[0])
    for cut in shards[1:]:
        level = level * one(*cut)
    return level


def bell_draw(key, shape, width, limit, cuts=(), kind=jnp.bfloat16):
    level = levels(key, shape, cuts, -0.22, 0.18) if cuts else 1.0
    entries = jax.random.normal(key, shape, jnp.float32) * width * level
    return jnp.minimum(jnp.maximum(entries, -limit), limit).astype(kind)


def setup_inputs(seed: int = 0) -> dict:
    key_of = jax.random.split(jax.random.key(seed), 8)
    solution = bell_draw(key_of[0], (NF, NPIX), 1.0, 6.0, ((0, 2), (1, 16)), jnp.float32)
    residual = draw_residual(jax.random.fold_in(key_of[7], 71), 0)
    direction = draw_direction(jax.random.fold_in(key_of[7], 71), 0)
    sidereal = jnp.clip(jax.random.uniform(key_of[3], (NSEG,), jnp.float32, -3.140625, 3.140625), -3.140625, 3.140625)
    response = jnp.clip(jnp.exp(math.log(0.3) - 2.3025852 * jax.random.uniform(key_of[4], (NSEG, WINPIX), jnp.float32) ** levels(key_of[4], (NSEG, WINPIX), ((0, 16),), -0.2, 0.2)), 0.03, 0.3)
    significant = draw_significant(jax.random.fold_in(key_of[7], 71), 0)
    inv_noise = jnp.clip(jnp.exp(math.log(4.0) - 2.7725887 * jax.random.uniform(key_of[6], (NSEG, NF), jnp.float32) ** levels(key_of[6], (NSEG, NF), ((0, 16), (1, 2)), -0.2, 0.2)), 0.25, 4.0)
    return {"solution": solution, "residual": residual, "direction": direction, "sidereal": sidereal, "response": response, "significant": significant, "inv_noise": inv_noise}


TWO_PI = 6.283185307179586
HALF_TURN = 3.141592653589793
baseline_x = -0.0060
baseline_y = 0.0070
baseline_z = 0.0035
low_freq = 20.0
bin_width = 0.25
epsilon = 1e-6


def pixel_angles(pixel_ids, columns):
    column = (pixel_ids // NDEC).astype(jnp.float32)
    dec_row = (pixel_ids % NDEC).astype(jnp.float32)
    right_asc = TWO_PI * (column + 0.5) / columns
    declin = HALF_TURN * ((dec_row + 0.5) / NDEC - 0.5)
    return right_asc, declin


def phase_tiles(sid_angle, weight, right_asc, declin, frequency):
    hour_angle = right_asc - sid_angle
    cos_dec = jnp.cos(declin)
    delays = baseline_x * cos_dec * jnp.cos(hour_angle) + baseline_y * cos_dec * jnp.sin(hour_angle) + baseline_z * jnp.sin(declin)
    phases = (TWO_PI * frequency)[:, None] * delays[None, :]
    return weight[None, :] * jnp.cos(phases), weight[None, :] * jnp.sin(phases)


def pixel_weights(response, significant):
    return response * jnp.repeat(significant.astype(jnp.float32), NDEC, axis=1)


def segment_images(sid_angles, weights, noise_rows, window, right_asc, declin, frequency):
    def one_segment(running, segment_items):
        sid_angle, weight, noise_row = segment_items
        cos_tile, sin_tile = phase_tiles(sid_angle, weight, right_asc, declin, frequency)
        fwd_real = jnp.sum(cos_tile * window, axis=1)
        fwd_imag = jnp.sum(sin_tile * window, axis=1)
        return running + cos_tile * (noise_row * fwd_real)[:, None] + sin_tile * (noise_row * fwd_imag)[:, None], None

    summed, _ = lax.scan(one_segment, jnp.zeros(window.shape, jnp.float32), (sid_angles, weights, noise_rows))
    return summed


def reference(solution, residual, direction, sidereal, response, significant, inv_noise):
    columns = RA_DEV * N_RA
    frequency = low_freq + bin_width * jnp.arange(NF, dtype=jnp.int32).astype(jnp.float32)
    offsets = jnp.arange(WINPIX, dtype=jnp.int32)

    def block_step(image, block_id):
        pixel_ids = jnp.mod((block_id - 2) * PIX_DEV + offsets, NPIX).astype(jnp.int32)
        right_asc, declin = pixel_angles(pixel_ids, columns)
        window = jnp.take(direction, pixel_ids, axis=1)
        start = (block_id * SEG_DEV).astype(jnp.int32)
        sid_angles = lax.dynamic_slice_in_dim(sidereal, start, SEG_DEV, 0)
        resp_rows = lax.dynamic_slice_in_dim(response, start, SEG_DEV, 0)
        kept_rows = lax.dynamic_slice_in_dim(significant, start, SEG_DEV, 0)
        noise_rows = lax.dynamic_slice_in_dim(inv_noise, start, SEG_DEV, 0)
        summed = segment_images(sid_angles, pixel_weights(resp_rows, kept_rows), noise_rows, window, right_asc, declin, frequency)
        return image.at[:, pixel_ids].add(summed), None

    image, _ = lax.scan(block_step, jnp.zeros((NF, NPIX), jnp.float32), jnp.arange(N_RA, dtype=jnp.int32))
    norm_now = jnp.sum(residual * residual) + epsilon
    alpha = norm_now / (jnp.sum(direction * image) + epsilon)
    solution_next = solution + alpha * direction
    residual_next = residual - alpha * image
    beta = jnp.sum(residual_next * residual_next) / norm_now
    return solution_next, residual_next, residual_next + beta * direction
```

```python
import functools
import math

import jax
import jax.numpy as jnp
import numpy as np
from jax import lax
from jax.experimental import pallas as pl
from jax.experimental.pallas import tpu as pltpu
from jax.sharding import PartitionSpec as P

NDEC = 64
RA_DEV = 2
SPAN = 256

TWO_PI = 6.283185307179586
baseline_x = -0.006
baseline_y = 0.007
baseline_z = 0.0035
low_freq = 20.0
bin_width = 0.25
epsilon = 1e-06
MESH = pl.DeviceIdType.MESH
OFFSETS = (-2, -1, 1, 2)


def poly_fit(function, high, degree):
    fit = np.polynomial.chebyshev.Chebyshev.interpolate(function, degree, domain=[0.0, high])
    return [float(c) for c in fit.convert(kind=np.polynomial.Polynomial).coef]


def sinc_turns(z):
    r = np.sqrt(z)
    return 2 * np.pi * np.sinc(2 * r)


COS_COEF = poly_fit(lambda z: np.cos(2 * np.pi * np.sqrt(z)), 0.25, 9)
SIN_COEF = poly_fit(sinc_turns, 0.25, 8)


def horner(coef, z):
    total = jnp.full_like(z, coef[-1])
    for c in coef[-2::-1]:
        total = total * z + c
    return total


def reduce_turns(p):
    return p - jnp.floor(p + 0.5)


def cos_turns(p):
    r = reduce_turns(p)
    return horner(COS_COEF, r * r)


def sincos_turns(p):
    r = reduce_turns(p)
    z = r * r
    return r * horner(SIN_COEF, z), horner(COS_COEF, z)


def node_count():
    reach = math.sqrt(baseline_x**2 + baseline_y**2 + baseline_z**2)
    c = math.pi * bin_width * SPAN * reach
    count = 2
    while 2 * (c / 2) ** count / math.factorial(count) > 3e-8:
        count += 2
    return count


def lagrange_rows(count):
    half = (SPAN - 1) / 2
    nodes = np.cos(np.pi * (2 * np.arange(count) + 1) / (2 * count))
    x = (np.arange(SPAN) - half) / half
    rows = []
    for r in range(count):
        row = np.ones(SPAN)
        for j in range(count):
            if j != r:
                row = row * (x - nodes[j]) / (nodes[r] - nodes[j])
        rows.append(row)
    return nodes, np.stack(rows).astype(np.float32)


def split(x):
    high = x.astype(jnp.bfloat16)
    return high, (x - high.astype(jnp.float32)).astype(jnp.bfloat16)


def kernel(
    n, m, nodes,
    sid_ref, resp_ref, sig_ref, noise_ref, lag_ref, dir_ref, res_ref,
    img_ref, ab_ref,
    asend, abuf, fsend, fbuf, gsend, gbuf, vh_ref, vl_ref, dsend, dbuf, esend, ebuf,
    a_ss, a_rs, b_ss, b_rs, c_ss, c_rs, d_ss, d_rs, e_ss, e_rs,
):
    me = lax.axis_index("ra")
    band = lax.axis_index("freq")
    count = len(nodes)
    seg = resp_ref.shape[0]
    pix = dir_ref.shape[1]
    bins = dir_ref.shape[0]
    chunks = [(k, min(k + SPAN, bins)) for k in range(0, bins, SPAN)]

    def ra_of(d):
        return lax.rem(me + d + n, n)

    barrier = pltpu.get_barrier_semaphore()
    for d in range(1, n):
        pl.semaphore_signal(barrier, inc=1, device_id={"ra": ra_of(d)}, device_id_type=MESH)
    for d in range(1, m):
        pl.semaphore_signal(
            barrier, inc=1, device_id={"freq": lax.rem(band + d, m)}, device_id_type=MESH
        )

    lane = lax.broadcasted_iota(jnp.int32, (seg, pix), 1)
    for g in range(5):
        kept = jnp.zeros((seg, pix), jnp.float32)
        for j in range(RA_DEV):
            col = jnp.broadcast_to(
                sig_ref[:, g * RA_DEV + j : g * RA_DEV + j + 1].astype(jnp.float32), (seg, pix)
            )
            kept = jnp.where(lane // NDEC == j, col, kept)
        w = resp_ref[:, g * pix : (g + 1) * pix] * kept
        asend[g, 0:seg, :] = w
        asend[g, seg : 2 * seg, :] = w
        for s in range(2 * seg):
            asend[g, 2 * seg + s : 2 * seg + s + 1, :] = jnp.full((1, pix), sid_ref[s % seg])
    abuf[2] = asend[2]
    dh, dl = split(dir_ref[...])
    dcat = jnp.concatenate([dh, dh, dl], axis=1)
    residual = res_ref[...]
    rr = jnp.sum(residual * residual, axis=0, keepdims=True)

    pl.semaphore_wait(barrier, n - 1 + m - 1)

    def remote(src, dst, ss, rs, where):
        return pltpu.make_async_remote_copy(
            src_ref=src, dst_ref=dst, send_sem=ss, recv_sem=rs, device_id=where, device_id_type=MESH
        )

    a_copies = []
    for d in OFFSETS:
        g = d + 2
        cp = remote(asend.at[g], abuf.at[g], a_ss.at[g], a_rs.at[g], {"ra": ra_of(d)})
        cp.start()
        a_copies.append(cp)

    lane1 = lax.broadcasted_iota(jnp.int32, (1, pix), 1)
    column = (me * RA_DEV + lane1 // NDEC).astype(jnp.float32)
    dec_row = (lane1 % NDEC).astype(jnp.float32)
    ra_turns = (column + 0.5) / (RA_DEV * n)
    sin_dec, cos_dec = sincos_turns(0.5 * ((dec_row + 0.5) / NDEC - 0.5))

    for cp in a_copies:
        cp.wait()

    rows = 10 * seg
    weight = jnp.concatenate([abuf[g, 0 : 2 * seg, :] for g in range(5)], axis=0)
    sid = jnp.concatenate([abuf[g, 2 * seg : 4 * seg, :] for g in range(5)], axis=0)
    sin_h, cos_h = sincos_turns(ra_turns - sid * (1.0 / TWO_PI))
    delay = cos_dec * (baseline_x * cos_h + baseline_y * sin_h) + baseline_z * sin_dec
    row_id = lax.broadcasted_iota(jnp.int32, (rows, pix), 0)
    shift = jnp.where(lax.rem(row_id, 2 * seg) >= seg, 0.25, 0.0)
    half = bin_width * (SPAN - 1) / 2
    fine = [sincos_turns((half * float(nodes[r])) * delay) for r in range(count // 2)]

    for index, (k0, k1) in enumerate(chunks):
        centre = low_freq + bin_width * (
            (band * bins + k0).astype(jnp.float32) + (SPAN - 1) / 2
        )
        p = reduce_turns(centre * delay)
        t0 = weight * cos_turns(p - shift)
        t1 = weight * cos_turns(p - shift + 0.25)
        up, down = [], []
        for sin_d, cos_d in fine:
            a, b = t0 * cos_d, t1 * sin_d
            up.append(a + b)
            down.append(a - b)
        table = jnp.concatenate(up + down[::-1], axis=0)
        vh, vl = split(table)
        vh_ref[index] = vh
        vl_ref[index] = vl
        product = lax.dot_general(
            jnp.concatenate([vh, vl, vh], axis=1), dcat[k0:k1],
            (((1,), (1,)), ((), ())), preferred_element_type=jnp.float32,
        )
        total = lag_ref[0:1, 0 : k1 - k0] * product[0:rows]
        for r in range(1, count):
            total = total + lag_ref[r : r + 1, 0 : k1 - k0] * product[r * rows : (r + 1) * rows]
        for g in range(5):
            fsend[g, :, k0:k1] = total[g * 2 * seg : (g + 1) * 2 * seg]

    b_copies = []
    for d in OFFSETS:
        g = d + 2
        cp = remote(fsend.at[g], fbuf.at[g], b_ss.at[g], b_rs.at[g], {"ra": ra_of(-d)})
        cp.start()
        b_copies.append(cp)
    noise = jnp.concatenate([noise_ref[...], noise_ref[...]], axis=0)
    for cp in b_copies:
        cp.wait()
    forward = fsend[2]
    for d in OFFSETS:
        forward = forward + fbuf[d + 2]
    weighted = noise * forward
    gsend[...] = weighted
    c_copies = []
    for d in OFFSETS:
        g = d + 2
        cp = remote(gsend, gbuf.at[g], c_ss.at[g], c_rs.at[g], {"ra": ra_of(d)})
        cp.start()
        c_copies.append(cp)
    gbuf[2] = weighted
    power = jnp.sum(weighted * forward)
    for cp in c_copies:
        cp.wait()

    cross = jnp.zeros((1, pix), jnp.float32)
    norm = jnp.zeros((1, pix), jnp.float32)
    for index, (k0, k1) in enumerate(chunks):
        g = jnp.concatenate([gbuf[j, :, k0:k1] for j in range(5)], axis=0)
        spread = jnp.concatenate(
            [lag_ref[r : r + 1, 0 : k1 - k0] * g for r in range(count)], axis=0
        )
        gh, gl = split(spread)
        vh, vl = vh_ref[index], vl_ref[index]
        image_t = lax.dot_general(
            jnp.concatenate([vh, vl, vh], axis=0), jnp.concatenate([gh, gh, gl], axis=0),
            (((0,), (0,)), ((), ())), preferred_element_type=jnp.float32,
        )
        image = image_t.T
        img_ref[k0:k1, :] = image
        cross = cross + jnp.sum(image * res_ref[k0:k1, :], axis=0, keepdims=True)
        norm = norm + jnp.sum(image * image, axis=0, keepdims=True)

    dsend[0:1, :] = rr
    dsend[1:2, :] = jnp.where(lane1 == 0, power, 0.0)
    dsend[2:3, :] = cross
    dsend[3:4, :] = norm
    dsend[4:8, :] = jnp.zeros((4, pix), jnp.float32)
    d_copies = []
    for d in range(1, m):
        cp = remote(
            dsend, dbuf.at[d], d_ss.at[d], d_rs.at[d], {"freq": lax.rem(band + d, m)}
        )
        cp.start()
        d_copies.append(cp)
    for cp in d_copies:
        cp.wait()
    sums = dsend[...]
    for d in range(1, m):
        sums = sums + dbuf[d]
    esend[...] = sums
    e_copies = []
    for d in range(1, n):
        cp = remote(esend, ebuf.at[d], e_ss.at[d], e_rs.at[d], {"ra": ra_of(d)})
        cp.start()
        e_copies.append(cp)
    for cp in e_copies:
        cp.wait()
    for d in range(1, n):
        sums = sums + ebuf[d]
    sums = jnp.sum(sums, axis=1, keepdims=True)
    rr_all, power_all, cross_all, norm_all = (sums[i : i + 1] for i in range(4))
    alpha = (rr_all + epsilon) / (power_all + epsilon)
    beta = (rr_all - 2.0 * alpha * cross_all + alpha * alpha * norm_all) / (rr_all + epsilon)
    ab_ref[0:1, :] = jnp.broadcast_to(alpha, (1, pix))
    ab_ref[1:2, :] = jnp.broadcast_to(beta, (1, pix))
    ab_ref[2:8, :] = jnp.zeros((6, pix), jnp.float32)


def solution(mesh):
    n, m = mesh.shape["ra"], mesh.shape["freq"]

    def shards(estimate, residual, direction, sidereal, response, significant, inv_noise):
        bins, pix = direction.shape
        seg = sidereal.shape[0]
        count = node_count()
        nodes, lagrange = lagrange_rows(count)
        pieces = -(-bins // SPAN)
        f32, bf16 = jnp.float32, jnp.bfloat16
        vmem = pl.BlockSpec(memory_space=pltpu.VMEM)
        dma = pltpu.SemaphoreType.DMA
        image, steps = pl.pallas_call(
            functools.partial(kernel, n, m, nodes),
            out_shape=(
                jax.ShapeDtypeStruct((bins, pix), f32),
                jax.ShapeDtypeStruct((8, pix), f32),
            ),
            in_specs=[pl.BlockSpec(memory_space=pltpu.SMEM)] + [vmem] * 6,
            out_specs=(vmem, vmem),
            scratch_shapes=[
                pltpu.VMEM((5, 4 * seg, pix), f32),
                pltpu.VMEM((5, 4 * seg, pix), f32),
                pltpu.VMEM((5, 2 * seg, bins), f32),
                pltpu.VMEM((5, 2 * seg, bins), f32),
                pltpu.VMEM((2 * seg, bins), f32),
                pltpu.VMEM((5, 2 * seg, bins), f32),
                pltpu.VMEM((pieces, count * 10 * seg, pix), bf16),
                pltpu.VMEM((pieces, count * 10 * seg, pix), bf16),
                pltpu.VMEM((8, pix), f32),
                pltpu.VMEM((m, 8, pix), f32),
                pltpu.VMEM((8, pix), f32),
                pltpu.VMEM((n, 8, pix), f32),
            ]
            + [dma((5,))] * 6
            + [dma((m,))] * 2
            + [dma((n,))] * 2,
            compiler_params=pltpu.CompilerParams(collective_id=0, has_side_effects=True),
        )(sidereal, response, significant, inv_noise, jnp.asarray(lagrange), direction, residual)
        alpha, beta = steps[0, 0], steps[1, 0]
        residual_next = residual - alpha * image
        return (
            estimate + alpha * direction,
            residual_next,
            residual_next + beta * direction,
        )

    return jax.shard_map(
        shards,
        mesh=mesh,
        in_specs=(
            P("freq", "ra"),
            P("freq", "ra"),
            P("freq", "ra"),
            P("ra"),
            P("ra", None),
            P("ra", None),
            P("ra", "freq"),
        ),
        out_specs=(P("freq", "ra"), P("freq", "ra"), P("freq", "ra")),
        check_vma=False,
    )
```

```python
import functools
import math

import jax
import jax.numpy as jnp
import numpy as np
from jax import lax
from jax.experimental import pallas as pl
from jax.experimental.pallas import tpu as pltpu
from jax.sharding import PartitionSpec as P

NDEC = 64
RA_DEV = 2
SPAN = 256

TWO_PI = 6.283185307179586
baseline_x = -0.006
baseline_y = 0.007
baseline_z = 0.0035
low_freq = 20.0
bin_width = 0.25
epsilon = 1e-06
MESH = pl.DeviceIdType.MESH
OFFSETS = (-2, -1, 1, 2)
UNROLL = 64


def poly_fit(function, high, degree):
    fit = np.polynomial.chebyshev.Chebyshev.interpolate(function, degree, domain=[0.0, high])
    return [float(c) for c in fit.convert(kind=np.polynomial.Polynomial).coef]


def sinc_turns(z):
    r = np.sqrt(z)
    return 2 * np.pi * np.sinc(2 * r)


COS_COEF = poly_fit(lambda z: np.cos(2 * np.pi * np.sqrt(z)), 0.25, 9)
SIN_COEF = poly_fit(sinc_turns, 0.25, 8)


def horner(coef, z):
    total = jnp.full_like(z, coef[-1])
    for c in coef[-2::-1]:
        total = total * z + c
    return total


def reduce_turns(p):
    return p - jnp.floor(p + 0.5)


def cos_turns(p):
    r = reduce_turns(p)
    return horner(COS_COEF, r * r)


def sincos_turns(p):
    r = reduce_turns(p)
    z = r * r
    return r * horner(SIN_COEF, z), horner(COS_COEF, z)


def node_count():
    reach = math.sqrt(baseline_x**2 + baseline_y**2 + baseline_z**2)
    c = math.pi * bin_width * SPAN * reach
    count = 2
    while 2 * (c / 2) ** count / math.factorial(count) > 3e-8:
        count += 2
    return count


def lagrange_rows(count):
    half = (SPAN - 1) / 2
    nodes = np.cos(np.pi * (2 * np.arange(count) + 1) / (2 * count))
    x = (np.arange(SPAN) - half) / half
    rows = []
    for r in range(count):
        row = np.ones(SPAN)
        for j in range(count):
            if j != r:
                row = row * (x - nodes[j]) / (nodes[r] - nodes[j])
        rows.append(row)
    return nodes, np.stack(rows).astype(np.float32)


def split(x):
    high = x.astype(jnp.bfloat16)
    return high, (x - high.astype(jnp.float32)).astype(jnp.bfloat16)


def kernel(
    n, m, nodes,
    sid_hbm, resp_hbm, sig_hbm, noise_hbm, lag_hbm, dir_hbm, res_hbm, est_hbm,
    sol_out, res_out, dir_out,
    sid_ref, resp_ref, sig_ref, noise_ref, lag_ref, dir_ref, res_ref, est_ref,
    asend, abuf, fsend, fbuf, gsend, gbuf, vh_ref, vl_ref, psend, pbuf, esend, ebuf,
    in_s, a_ss, a_rs, b_ss, b_rs, c_ss, c_rs, p_ss, p_rs, e_ss, e_rs,
):
    me = lax.axis_index("ra")
    band = lax.axis_index("freq")
    count = len(nodes)
    seg = resp_ref.shape[0]
    pix = dir_ref.shape[1]
    bins = dir_ref.shape[0]
    chunks = [(k, min(k + SPAN, bins)) for k in range(0, bins, SPAN)]
    everyone = n * m

    def ra_of(d):
        return lax.rem(me + d + n, n)

    def peer(i):
        return {"ra": lax.rem(me + i // m, n), "freq": lax.rem(band + i % m, m)}

    def each_peer(action):
        if everyone <= UNROLL:
            for i in range(1, everyone):
                action(i)
        else:
            @pl.loop(1, everyone)
            def _(i):
                action(i)

    barrier = pltpu.get_barrier_semaphore()
    each_peer(
        lambda i: pl.semaphore_signal(barrier, inc=1, device_id=peer(i), device_id_type=MESH)
    )
    pairs = [
        (resp_hbm, resp_ref), (sig_hbm, sig_ref), (sid_hbm, sid_ref), (dir_hbm, dir_ref),
        (lag_hbm, lag_ref), (res_hbm, res_ref), (noise_hbm, noise_ref), (est_hbm, est_ref),
    ]
    loads = [pltpu.make_async_copy(a, b, in_s.at[j]) for j, (a, b) in enumerate(pairs)]
    for cp in loads:
        cp.start()
    tail = chunks[-1][1] - chunks[-1][0]
    if tail < SPAN:
        fsend[len(chunks) - 1] = jnp.zeros(fsend.shape[1:], jnp.float32)
        gsend[len(chunks) - 1] = jnp.zeros(gsend.shape[1:], jnp.float32)

    lane1 = lax.broadcasted_iota(jnp.int32, (1, pix), 1)
    column = (me * RA_DEV + lane1 // NDEC).astype(jnp.float32)
    dec_row = (lane1 % NDEC).astype(jnp.float32)
    ra_turns = (column + 0.5) / (RA_DEV * n)
    sin_dec, cos_dec = sincos_turns(0.5 * ((dec_row + 0.5) / NDEC - 0.5))

    for cp in loads[:3]:
        cp.wait()
    lane = lax.broadcasted_iota(jnp.int32, (seg, pix), 1)
    for g in range(5):
        kept = jnp.zeros((seg, pix), jnp.float32)
        for j in range(RA_DEV):
            col = jnp.broadcast_to(
                sig_ref[:, g * RA_DEV + j : g * RA_DEV + j + 1].astype(jnp.float32), (seg, pix)
            )
            kept = jnp.where(lane // NDEC == j, col, kept)
        w = resp_ref[:, g * pix : (g + 1) * pix] * kept
        asend[g, 0:seg, :] = w
        asend[g, seg : 2 * seg, :] = w
        for s in range(2 * seg):
            asend[g, 2 * seg + s : 2 * seg + s + 1, :] = jnp.full((1, pix), sid_ref[s % seg])
    abuf[2] = asend[2]
    for cp in loads[3:6]:
        cp.wait()
    dh, dl = split(dir_ref[...])
    dcat = jnp.concatenate([dh, dh, dl], axis=1)
    residual = res_ref[...]
    rr = jnp.sum(residual * residual, axis=0, keepdims=True)

    pl.semaphore_wait(barrier, everyone - 1)

    def remote(src, dst, ss, rs, where):
        return pltpu.make_async_remote_copy(
            src_ref=src, dst_ref=dst, send_sem=ss, recv_sem=rs, device_id=where, device_id_type=MESH
        )

    a_copies = []
    for d in OFFSETS:
        g = d + 2
        cp = remote(asend.at[g], abuf.at[g], a_ss.at[g], a_rs.at[g], {"ra": ra_of(d)})
        cp.start()
        a_copies.append(cp)
    for cp in loads[6:]:
        cp.wait()
    noise = jnp.concatenate([noise_ref[...], noise_ref[...]], axis=0)
    for cp in a_copies:
        cp.wait_recv()

    rows = 10 * seg
    weight = jnp.concatenate([abuf[g, 0 : 2 * seg, :] for g in range(5)], axis=0)
    sid = jnp.concatenate([abuf[g, 2 * seg : 4 * seg, :] for g in range(5)], axis=0)
    sin_h, cos_h = sincos_turns(ra_turns - sid * (1.0 / TWO_PI))
    delay = cos_dec * (baseline_x * cos_h + baseline_y * sin_h) + baseline_z * sin_dec
    row_id = lax.broadcasted_iota(jnp.int32, (rows, pix), 0)
    shift = jnp.where(lax.rem(row_id, 2 * seg) >= seg, 0.25, 0.0)
    half = bin_width * (SPAN - 1) / 2
    fine = [sincos_turns((half * float(nodes[r])) * delay) for r in range(count // 2)]

    b_copies = []
    for index, (k0, k1) in enumerate(chunks):
        centre = low_freq + bin_width * (
            (band * bins + k0).astype(jnp.float32) + (SPAN - 1) / 2
        )
        p = reduce_turns(centre * delay)
        t0 = weight * cos_turns(p - shift)
        t1 = weight * cos_turns(p - shift + 0.25)
        up, down = [], []
        for sin_d, cos_d in fine:
            a, b = t0 * cos_d, t1 * sin_d
            up.append(a + b)
            down.append(a - b)
        table = jnp.concatenate(up + down[::-1], axis=0)
        vh, vl = split(table)
        vh_ref[index] = vh
        vl_ref[index] = vl
        product = lax.dot_general(
            jnp.concatenate([vh, vl, vh], axis=1), dcat[k0:k1],
            (((1,), (1,)), ((), ())), preferred_element_type=jnp.float32,
        )
        total = lag_ref[0:1, 0 : k1 - k0] * product[0:rows]
        for r in range(1, count):
            total = total + lag_ref[r : r + 1, 0 : k1 - k0] * product[r * rows : (r + 1) * rows]
        for g in range(5):
            fsend[index, g, :, 0 : k1 - k0] = total[g * 2 * seg : (g + 1) * 2 * seg]
        for d in OFFSETS:
            g = d + 2
            cp = remote(
                fsend.at[index, g], fbuf.at[index, g],
                b_ss.at[index, g], b_rs.at[index, g], {"ra": ra_of(-d)},
            )
            cp.start()
            b_copies.append(cp)

    c_copies = []
    power = jnp.zeros((1, pix), jnp.float32)
    for index, (k0, k1) in enumerate(chunks):
        for cp in b_copies[index * 4 : index * 4 + 4]:
            cp.wait_recv()
        forward = fsend[index, 2, :, 0 : k1 - k0]
        for d in OFFSETS:
            forward = forward + fbuf[index, d + 2, :, 0 : k1 - k0]
        weighted = noise[:, k0:k1] * forward
        gsend[index, :, 0 : k1 - k0] = weighted
        for d in OFFSETS:
            g = d + 2
            cp = remote(
                gsend.at[index], gbuf.at[index, g],
                c_ss.at[index, g], c_rs.at[index, g], {"ra": ra_of(d)},
            )
            cp.start()
            c_copies.append(cp)
        gbuf[index, 2, :, 0 : k1 - k0] = weighted
        both = jnp.sum(weighted * forward, axis=0, keepdims=True)
        for q in range(0, k1 - k0, pix):
            piece = both[:, q : min(q + pix, k1 - k0)]
            if piece.shape[1] < pix:
                piece = jnp.concatenate(
                    [piece, jnp.zeros((1, pix - piece.shape[1]), jnp.float32)], axis=1
                )
            power = power + piece
    psend[0:1, 0:pix] = rr
    psend[0:1, pix : 2 * pix] = power

    def share(src, buf, ss, rs):
        each_peer(lambda i: remote(src, buf.at[i], ss.at[i], rs.at[i], peer(i)).start())

    def gathered(src, buf, ss, rs):
        each_peer(lambda i: remote(src, buf.at[i], ss.at[i], rs.at[i], peer(i)).wait_recv())
        return jnp.sum(buf[...], axis=0)

    def sent(src, buf, ss, rs):
        each_peer(lambda i: remote(src, buf.at[i], ss.at[i], rs.at[i], peer(i)).wait_send())

    pbuf[0] = psend[...]
    share(psend, pbuf, p_ss, p_rs)

    images = []
    for index, (k0, k1) in enumerate(chunks):
        for cp in c_copies[index * 4 : index * 4 + 4]:
            cp.wait_recv()
        g = jnp.concatenate([gbuf[index, j, :, 0 : k1 - k0] for j in range(5)], axis=0)
        spread = jnp.concatenate(
            [lag_ref[r : r + 1, 0 : k1 - k0] * g for r in range(count)], axis=0
        )
        gh, gl = split(spread)
        vh, vl = vh_ref[index], vl_ref[index]
        image_t = lax.dot_general(
            jnp.concatenate([vh, vl, vh], axis=0), jnp.concatenate([gh, gh, gl], axis=0),
            (((0,), (0,)), ((), ())), preferred_element_type=jnp.float32,
        )
        res_out[k0:k1, :] = image_t.T

    totals = gathered(psend, pbuf, p_ss, p_rs)
    rr_all = jnp.sum(totals[:, 0:pix], axis=1, keepdims=True) + epsilon
    alpha = rr_all / (jnp.sum(totals[:, pix : 2 * pix], axis=1, keepdims=True) + epsilon)
    residual_next = res_ref[...] - alpha * res_out[...]
    res_out[...] = residual_next
    norm = jnp.sum(residual_next * residual_next, axis=0, keepdims=True)
    esend[...] = norm
    ebuf[0] = norm
    share(esend, ebuf, e_ss, e_rs)
    sol_out[...] = est_ref[...] + alpha * dir_ref[...]
    for cp in a_copies + b_copies + c_copies:
        cp.wait_send()
    sent(psend, pbuf, p_ss, p_rs)
    norm_all = jnp.sum(gathered(esend, ebuf, e_ss, e_rs), axis=1, keepdims=True)
    beta = norm_all / rr_all
    dir_out[...] = res_out[...] + beta * dir_ref[...]
    sent(esend, ebuf, e_ss, e_rs)


def solution(mesh):
    n, m = mesh.shape["ra"], mesh.shape["freq"]

    def shards(estimate, residual, direction, sidereal, response, significant, inv_noise):
        bins, pix = direction.shape
        seg = sidereal.shape[0]
        count = node_count()
        nodes, lagrange = lagrange_rows(count)
        pieces = -(-bins // SPAN)
        f32, bf16 = jnp.float32, jnp.bfloat16
        vmem = pl.BlockSpec(memory_space=pltpu.VMEM)
        dma = pltpu.SemaphoreType.DMA
        operands = (
            sidereal, response, significant, inv_noise, jnp.asarray(lagrange),
            direction, residual, estimate,
        )
        return pl.pallas_call(
            functools.partial(kernel, n, m, nodes),
            out_shape=(jax.ShapeDtypeStruct((bins, pix), f32),) * 3,
            in_specs=[pl.BlockSpec(memory_space=pl.ANY)] * len(operands),
            out_specs=(vmem,) * 3,
            scratch_shapes=[pltpu.SMEM(sidereal.shape, f32)]
            + [pltpu.VMEM(x.shape, x.dtype) for x in operands[1:]]
            + [
                pltpu.VMEM((5, 4 * seg, pix), f32),
                pltpu.VMEM((5, 4 * seg, pix), f32),
                pltpu.VMEM((pieces, 5, 2 * seg, SPAN), f32),
                pltpu.VMEM((pieces, 5, 2 * seg, SPAN), f32),
                pltpu.VMEM((pieces, 2 * seg, SPAN), f32),
                pltpu.VMEM((pieces, 5, 2 * seg, SPAN), f32),
                pltpu.VMEM((pieces, count * 10 * seg, pix), bf16),
                pltpu.VMEM((pieces, count * 10 * seg, pix), bf16),
                pltpu.VMEM((1, 2 * pix), f32),
                pltpu.VMEM((n * m, 1, 2 * pix), f32),
                pltpu.VMEM((1, pix), f32),
                pltpu.VMEM((n * m, 1, pix), f32),
                dma((len(operands),)),
            ]
            + [dma((5,))] * 2
            + [dma((pieces, 5))] * 4
            + [dma((n * m,))] * 4,
            compiler_params=pltpu.CompilerParams(collective_id=0, has_side_effects=True),
        )(*operands)

    return jax.shard_map(
        shards,
        mesh=mesh,
        in_specs=(
            P("freq", "ra"),
            P("freq", "ra"),
            P("freq", "ra"),
            P("ra"),
            P("ra", None),
            P("ra", None),
            P("ra", "freq"),
        ),
        out_specs=(P("freq", "ra"), P("freq", "ra"), P("freq", "ra")),
        check_vma=False,
    )
```

```python
import functools
import math

import jax
import jax.numpy as jnp
import numpy as np
from jax import lax
from jax.experimental import pallas as pl
from jax.experimental.pallas import tpu as pltpu
from jax.sharding import PartitionSpec as P

NDEC = 64
RA_DEV = 2
SPAN = 256

TWO_PI = 6.283185307179586
baseline_x = -0.006
baseline_y = 0.007
baseline_z = 0.0035
low_freq = 20.0
bin_width = 0.25
epsilon = 1e-06
MESH = pl.DeviceIdType.MESH
OFFSETS = (-2, -1, 1, 2)
BATCHES = ((2, 3, 4), (0, 1))
UNROLL = 64


def poly_fit(function, high, degree):
    fit = np.polynomial.chebyshev.Chebyshev.interpolate(function, degree, domain=[0.0, high])
    return [float(c) for c in fit.convert(kind=np.polynomial.Polynomial).coef]


def sinc_turns(z):
    r = np.sqrt(z)
    return 2 * np.pi * np.sinc(2 * r)


COS_COEF = poly_fit(lambda z: np.cos(2 * np.pi * np.sqrt(z)), 0.25, 9)
SIN_COEF = poly_fit(sinc_turns, 0.25, 8)


def horner(coef, z):
    total = jnp.full_like(z, coef[-1])
    for c in coef[-2::-1]:
        total = total * z + c
    return total


def reduce_turns(p):
    return p - jnp.floor(p + 0.5)


def cos_turns(p):
    r = reduce_turns(p)
    return horner(COS_COEF, r * r)


def sincos_turns(p):
    r = reduce_turns(p)
    z = r * r
    return r * horner(SIN_COEF, z), horner(COS_COEF, z)


def node_count():
    reach = math.sqrt(baseline_x**2 + baseline_y**2 + baseline_z**2)
    c = math.pi * bin_width * SPAN * reach
    count = 2
    while 2 * (c / 2) ** count / math.factorial(count) > 3e-8:
        count += 2
    return count


def lagrange_rows(count):
    half = (SPAN - 1) / 2
    nodes = np.cos(np.pi * (2 * np.arange(count) + 1) / (2 * count))
    x = (np.arange(SPAN) - half) / half
    rows = []
    for r in range(count):
        row = np.ones(SPAN)
        for j in range(count):
            if j != r:
                row = row * (x - nodes[j]) / (nodes[r] - nodes[j])
        rows.append(row)
    return nodes, np.stack(rows).astype(np.float32)


def split(x):
    high = x.astype(jnp.bfloat16)
    return high, (x - high.astype(jnp.float32)).astype(jnp.bfloat16)


def kernel(
    n, m, nodes,
    sid_hbm, resp_hbm, sig_hbm, noise_hbm, lag_hbm, dir_hbm, res_hbm, est_hbm,
    sol_out, res_out, dir_out,
    sid_ref, resp_ref, sig_ref, noise_ref, lag_ref, dir_ref, res_ref, est_ref,
    asend, abuf, fsend, fbuf, gsend, gbuf, vh_refs, vl_refs, image_ref, psend, pbuf, esend, ebuf,
    in_s, a_ss, a_rs, b_ss, b_rs, c_ss, c_rs, p_ss, p_rs, e_ss, e_rs,
):
    me = lax.axis_index("ra")
    band = lax.axis_index("freq")
    count = len(nodes)
    seg = resp_ref.shape[0]
    pix = dir_ref.shape[1]
    bins = dir_ref.shape[0]
    chunks = [(k, min(k + SPAN, bins)) for k in range(0, bins, SPAN)]
    everyone = n * m

    def ra_of(d):
        return lax.rem(me + d + n, n)

    def peer(i):
        return {"ra": lax.rem(me + i // m, n), "freq": lax.rem(band + i % m, m)}

    def each_peer(action):
        if everyone <= UNROLL:
            order = sorted(range(1, everyone), key=lambda i: min(i // m, n - i // m))
            for i in order:
                action(i)
        else:
            @pl.loop(1, everyone)
            def _(i):
                action(i)

    barrier = pltpu.get_barrier_semaphore()
    each_peer(
        lambda i: pl.semaphore_signal(barrier, inc=1, device_id=peer(i), device_id_type=MESH)
    )
    pairs = [
        (resp_hbm, resp_ref), (sig_hbm, sig_ref), (sid_hbm, sid_ref), (dir_hbm, dir_ref),
        (lag_hbm, lag_ref), (res_hbm, res_ref), (noise_hbm, noise_ref), (est_hbm, est_ref),
    ]
    loads = [pltpu.make_async_copy(a, b, in_s.at[j]) for j, (a, b) in enumerate(pairs)]
    for cp in loads:
        cp.start()
    tail = chunks[-1][1] - chunks[-1][0]
    if tail < SPAN:
        fsend[len(chunks) - 1] = jnp.zeros(fsend.shape[1:], jnp.float32)
        gsend[len(chunks) - 1] = jnp.zeros(gsend.shape[1:], jnp.float32)

    lane1 = lax.broadcasted_iota(jnp.int32, (1, pix), 1)
    column = (me * RA_DEV + lane1 // NDEC).astype(jnp.float32)
    dec_row = (lane1 % NDEC).astype(jnp.float32)
    ra_turns = (column + 0.5) / (RA_DEV * n)
    sin_dec, cos_dec = sincos_turns(0.5 * ((dec_row + 0.5) / NDEC - 0.5))

    for cp in loads[:3]:
        cp.wait()
    lane = lax.broadcasted_iota(jnp.int32, (seg, pix), 1)
    for g in range(5):
        kept = jnp.zeros((seg, pix), jnp.float32)
        for j in range(RA_DEV):
            col = jnp.broadcast_to(
                sig_ref[:, g * RA_DEV + j : g * RA_DEV + j + 1].astype(jnp.float32), (seg, pix)
            )
            kept = jnp.where(lane // NDEC == j, col, kept)
        w = resp_ref[:, g * pix : (g + 1) * pix] * kept
        asend[g, 0:seg, :] = w
        asend[g, seg : 2 * seg, :] = w
        for s in range(2 * seg):
            asend[g, 2 * seg + s : 2 * seg + s + 1, :] = jnp.full((1, pix), sid_ref[s % seg])
    abuf[2] = asend[2]
    for cp in loads[3:6]:
        cp.wait()
    dh, dl = split(dir_ref[...])
    dcat = jnp.concatenate([dh, dh, dl], axis=1)
    residual = res_ref[...]
    rr = jnp.sum(residual * residual, axis=0, keepdims=True)

    pl.semaphore_wait(barrier, everyone - 1)

    def remote(src, dst, ss, rs, where):
        return pltpu.make_async_remote_copy(
            src_ref=src, dst_ref=dst, send_sem=ss, recv_sem=rs, device_id=where, device_id_type=MESH
        )

    a_copies = []
    for d in OFFSETS:
        g = d + 2
        cp = remote(asend.at[g], abuf.at[g], a_ss.at[g], a_rs.at[g], {"ra": ra_of(d)})
        cp.start()
        a_copies.append(cp)
    for cp in loads[6:]:
        cp.wait()
    noise = jnp.concatenate([noise_ref[...], noise_ref[...]], axis=0)
    b_copies = {}
    for batch, groups in enumerate(BATCHES):
        for g in groups:
            if g != 2:
                a_copies[OFFSETS.index(g - 2)].wait_recv()
        rows = len(groups) * 2 * seg
        weight = jnp.concatenate([abuf[g, 0 : 2 * seg, :] for g in groups], axis=0)
        sid = jnp.concatenate([abuf[g, 2 * seg : 4 * seg, :] for g in groups], axis=0)
        sin_h, cos_h = sincos_turns(ra_turns - sid * (1.0 / TWO_PI))
        delay = cos_dec * (baseline_x * cos_h + baseline_y * sin_h) + baseline_z * sin_dec
        row_id = lax.broadcasted_iota(jnp.int32, (rows, pix), 0)
        shift = jnp.where(lax.rem(row_id, 2 * seg) >= seg, 0.25, 0.0)
        half = bin_width * (SPAN - 1) / 2
        fine = [sincos_turns((half * float(nodes[r])) * delay) for r in range(count // 2)]
        for index, (k0, k1) in enumerate(chunks):
            centre = low_freq + bin_width * (
                (band * bins + k0).astype(jnp.float32) + (SPAN - 1) / 2
            )
            p = reduce_turns(centre * delay)
            t0 = weight * cos_turns(p - shift)
            t1 = weight * cos_turns(p - shift + 0.25)
            up, down = [], []
            for sin_d, cos_d in fine:
                a, b = t0 * cos_d, t1 * sin_d
                up.append(a + b)
                down.append(a - b)
            table = jnp.concatenate(up + down[::-1], axis=0)
            vh, vl = split(table)
            vh_refs[batch][index] = vh
            vl_refs[batch][index] = vl
            product = lax.dot_general(
                jnp.concatenate([vh, vl, vh], axis=1), dcat[k0:k1],
                (((1,), (1,)), ((), ())), preferred_element_type=jnp.float32,
            )
            total = lag_ref[0:1, 0 : k1 - k0] * product[0:rows]
            for r in range(1, count):
                total = total + (
                    lag_ref[r : r + 1, 0 : k1 - k0] * product[r * rows : (r + 1) * rows]
                )
            for at, g in enumerate(groups):
                fsend[index, g, :, 0 : k1 - k0] = total[at * 2 * seg : (at + 1) * 2 * seg]
                if g != 2:
                    cp = remote(
                        fsend.at[index, g], fbuf.at[index, g],
                        b_ss.at[index, g], b_rs.at[index, g], {"ra": ra_of(2 - g)},
                    )
                    cp.start()
                    b_copies[index, g] = cp

    c_copies = {}
    power = jnp.zeros((1, pix), jnp.float32)
    for index, (k0, k1) in enumerate(chunks):
        for d in OFFSETS:
            b_copies[index, d + 2].wait_recv()
        forward = fsend[index, 2, :, 0 : k1 - k0]
        for d in OFFSETS:
            forward = forward + fbuf[index, d + 2, :, 0 : k1 - k0]
        weighted = noise[:, k0:k1] * forward
        gsend[index, :, 0 : k1 - k0] = weighted
        for d in OFFSETS:
            g = d + 2
            cp = remote(
                gsend.at[index], gbuf.at[index, g],
                c_ss.at[index, g], c_rs.at[index, g], {"ra": ra_of(d)},
            )
            cp.start()
            c_copies[index, g] = cp
        gbuf[index, 2, :, 0 : k1 - k0] = weighted
        both = jnp.sum(weighted * forward, axis=0, keepdims=True)
        for q in range(0, k1 - k0, pix):
            piece = both[:, q : min(q + pix, k1 - k0)]
            if piece.shape[1] < pix:
                piece = jnp.concatenate(
                    [piece, jnp.zeros((1, pix - piece.shape[1]), jnp.float32)], axis=1
                )
            power = power + piece
    psend[0:1, 0:pix] = rr
    psend[0:1, pix : 2 * pix] = power

    def share(src, buf, ss, rs):
        each_peer(lambda i: remote(src, buf.at[i], ss.at[i], rs.at[i], peer(i)).start())

    def gathered(src, buf, ss, rs):
        each_peer(lambda i: remote(src, buf.at[i], ss.at[i], rs.at[i], peer(i)).wait_recv())
        return jnp.sum(buf[...], axis=0)

    def sent(src, buf, ss, rs):
        each_peer(lambda i: remote(src, buf.at[i], ss.at[i], rs.at[i], peer(i)).wait_send())

    pbuf[0] = psend[...]
    share(psend, pbuf, p_ss, p_rs)

    cross = jnp.zeros((1, pix), jnp.float32)
    norm = jnp.zeros((1, pix), jnp.float32)
    for batch, groups in enumerate(BATCHES):
        for index, (k0, k1) in enumerate(chunks):
            for j in groups:
                if j != 2:
                    c_copies[index, j].wait_recv()
            g = jnp.concatenate([gbuf[index, j, :, 0 : k1 - k0] for j in groups], axis=0)
            spread = jnp.concatenate(
                [lag_ref[r : r + 1, 0 : k1 - k0] * g for r in range(count)], axis=0
            )
            gh, gl = split(spread)
            vh, vl = vh_refs[batch][index], vl_refs[batch][index]
            image_t = lax.dot_general(
                jnp.concatenate([vh, vl, vh], axis=0), jnp.concatenate([gh, gh, gl], axis=0),
                (((0,), (0,)), ((), ())), preferred_element_type=jnp.float32,
            )
            if batch == 0:
                image_ref[k0:k1, :] = image_t.T
            else:
                image = image_ref[k0:k1, :] + image_t.T
                image_ref[k0:k1, :] = image
                cross = cross + jnp.sum(image * res_ref[k0:k1, :], axis=0, keepdims=True)
                norm = norm + jnp.sum(image * image, axis=0, keepdims=True)

    esend[0:1, 0:pix] = cross
    esend[0:1, pix : 2 * pix] = norm
    ebuf[0] = esend[...]
    share(esend, ebuf, e_ss, e_rs)
    totals = gathered(psend, pbuf, p_ss, p_rs)
    rr_all = jnp.sum(totals[:, 0:pix], axis=1, keepdims=True)
    power_all = jnp.sum(totals[:, pix : 2 * pix], axis=1, keepdims=True)
    alpha = (rr_all + epsilon) / (power_all + epsilon)
    sol_out[...] = est_ref[...] + alpha * dir_ref[...]
    res_out[...] = res_ref[...] - alpha * image_ref[...]
    for cp in a_copies + list(b_copies.values()) + list(c_copies.values()):
        cp.wait_send()
    sent(psend, pbuf, p_ss, p_rs)
    totals = gathered(esend, ebuf, e_ss, e_rs)
    cross_all = jnp.sum(totals[:, 0:pix], axis=1, keepdims=True)
    norm_all = jnp.sum(totals[:, pix : 2 * pix], axis=1, keepdims=True)
    norm_next = rr_all - 2.0 * alpha * cross_all + alpha * alpha * norm_all
    beta = norm_next / (rr_all + epsilon)
    dir_out[...] = res_out[...] + beta * dir_ref[...]
    sent(esend, ebuf, e_ss, e_rs)


def solution(mesh):
    n, m = mesh.shape["ra"], mesh.shape["freq"]

    def shards(estimate, residual, direction, sidereal, response, significant, inv_noise):
        bins, pix = direction.shape
        seg = sidereal.shape[0]
        count = node_count()
        nodes, lagrange = lagrange_rows(count)
        pieces = -(-bins // SPAN)
        f32, bf16 = jnp.float32, jnp.bfloat16
        vmem = pl.BlockSpec(memory_space=pltpu.VMEM)
        dma = pltpu.SemaphoreType.DMA
        operands = (
            sidereal, response, significant, inv_noise, jnp.asarray(lagrange),
            direction, residual, estimate,
        )
        updated = pl.pallas_call(
            functools.partial(kernel, n, m, nodes),
            out_shape=(pltpu.VMEM((bins, pix), f32),) * 3,
            in_specs=[pl.BlockSpec(memory_space=pl.ANY)] * len(operands),
            out_specs=(vmem,) * 3,
            scratch_shapes=[pltpu.SMEM(sidereal.shape, f32)]
            + [pltpu.VMEM(x.shape, x.dtype) for x in operands[1:]]
            + [
                pltpu.VMEM((5, 4 * seg, pix), f32),
                pltpu.VMEM((5, 4 * seg, pix), f32),
                pltpu.VMEM((pieces, 5, 2 * seg, SPAN), f32),
                pltpu.VMEM((pieces, 5, 2 * seg, SPAN), f32),
                pltpu.VMEM((pieces, 2 * seg, SPAN), f32),
                pltpu.VMEM((pieces, 5, 2 * seg, SPAN), f32),
                [pltpu.VMEM((pieces, count * 2 * seg * len(b), pix), bf16) for b in BATCHES],
                [pltpu.VMEM((pieces, count * 2 * seg * len(b), pix), bf16) for b in BATCHES],
                pltpu.VMEM((bins, pix), f32),
                pltpu.VMEM((1, 2 * pix), f32),
                pltpu.VMEM((n * m, 1, 2 * pix), f32),
                pltpu.VMEM((1, 2 * pix), f32),
                pltpu.VMEM((n * m, 1, 2 * pix), f32),
                dma((len(operands),)),
            ]
            + [dma((5,))] * 2
            + [dma((pieces, 5))] * 4
            + [dma((n * m,))] * 4,
            compiler_params=pltpu.CompilerParams(collective_id=0, has_side_effects=True),
        )(*operands)
        return updated

    return jax.shard_map(
        shards,
        mesh=mesh,
        in_specs=(
            P("freq", "ra"),
            P("freq", "ra"),
            P("freq", "ra"),
            P("ra"),
            P("ra", None),
            P("ra", None),
            P("ra", "freq"),
        ),
        out_specs=(P("freq", "ra"), P("freq", "ra"), P("freq", "ra")),
        check_vma=False,
    )
```

```python
import functools
import math

import jax
import jax.numpy as jnp
import numpy as np
from jax import lax
from jax.experimental import pallas as pl
from jax.experimental.pallas import tpu as pltpu
from jax.sharding import PartitionSpec as P

NDEC = 64
RA_DEV = 2
SPAN = 256

TWO_PI = 6.283185307179586
baseline_x = -0.006
baseline_y = 0.007
baseline_z = 0.0035
low_freq = 20.0
bin_width = 0.25
epsilon = 1e-06
MESH = pl.DeviceIdType.MESH
OFFSETS = (-2, -1, 1, 2)
BATCHES = ((2, 3, 4), (0, 1))
UNROLL = 64


def poly_fit(function, high, degree):
    fit = np.polynomial.chebyshev.Chebyshev.interpolate(function, degree, domain=[0.0, high])
    return [float(c) for c in fit.convert(kind=np.polynomial.Polynomial).coef]


def sinc_turns(z):
    r = np.sqrt(z)
    return 2 * np.pi * np.sinc(2 * r)


COS_COEF = poly_fit(lambda z: np.cos(2 * np.pi * np.sqrt(z)), 0.25, 9)
SIN_COEF = poly_fit(sinc_turns, 0.25, 8)


def horner(coef, z):
    total = jnp.full_like(z, coef[-1])
    for c in coef[-2::-1]:
        total = total * z + c
    return total


def reduce_turns(p):
    return p - jnp.floor(p + 0.5)


def cos_turns(p):
    r = reduce_turns(p)
    return horner(COS_COEF, r * r)


def sincos_turns(p):
    r = reduce_turns(p)
    z = r * r
    return r * horner(SIN_COEF, z), horner(COS_COEF, z)


def node_count():
    reach = math.sqrt(baseline_x**2 + baseline_y**2 + baseline_z**2)
    c = math.pi * bin_width * SPAN * reach
    count = 2
    while 2 * (c / 2) ** count / math.factorial(count) > 3e-8:
        count += 2
    return count


def lagrange_rows(count):
    half = (SPAN - 1) / 2
    nodes = np.cos(np.pi * (2 * np.arange(count) + 1) / (2 * count))
    x = (np.arange(SPAN) - half) / half
    rows = []
    for r in range(count):
        row = np.ones(SPAN)
        for j in range(count):
            if j != r:
                row = row * (x - nodes[j]) / (nodes[r] - nodes[j])
        rows.append(row)
    return nodes, np.stack(rows).astype(np.float32)


def split(x):
    high = x.astype(jnp.bfloat16)
    return high, (x - high.astype(jnp.float32)).astype(jnp.bfloat16)


def kernel(
    n, m, nodes,
    sid_hbm, resp_hbm, sig_hbm, noise_hbm, lag_hbm, dir_hbm, res_hbm, est_hbm,
    sol_out, res_out, dir_out,
    sid_ref, resp_ref, sig_ref, noise_ref, lag_ref, dir_ref, res_ref, est_ref,
    asend, abuf, fsend, fbuf, gsend, gbuf, vh_refs, vl_refs, image_ref, psend, pbuf, esend, ebuf,
    in_s, a_ss, a_rs, b_ss, b_rs, c_ss, c_rs, p_ss, p_rs, e_ss, e_rs,
):
    me = lax.axis_index("ra")
    band = lax.axis_index("freq")
    count = len(nodes)
    seg = resp_ref.shape[0]
    pix = dir_ref.shape[1]
    bins = dir_ref.shape[0]
    chunks = [(k, min(k + SPAN, bins)) for k in range(0, bins, SPAN)]
    everyone = n * m

    def ra_of(d):
        return lax.rem(me + d + n, n)

    def peer(i):
        return {"ra": lax.rem(me + i // m, n), "freq": lax.rem(band + i % m, m)}

    def each_peer(action):
        if everyone <= UNROLL:
            order = sorted(range(1, everyone), key=lambda i: min(i // m, n - i // m))
            for i in order:
                action(i)
        else:
            @pl.loop(1, everyone)
            def _(i):
                action(i)

    barrier = pltpu.get_barrier_semaphore()
    each_peer(
        lambda i: pl.semaphore_signal(barrier, inc=1, device_id=peer(i), device_id_type=MESH)
    )
    pairs = [
        (resp_hbm, resp_ref), (sig_hbm, sig_ref), (sid_hbm, sid_ref), (dir_hbm, dir_ref),
        (lag_hbm, lag_ref), (res_hbm, res_ref), (noise_hbm, noise_ref), (est_hbm, est_ref),
    ]
    loads = [pltpu.make_async_copy(a, b, in_s.at[j]) for j, (a, b) in enumerate(pairs)]
    for cp in loads:
        cp.start()
    tail = chunks[-1][1] - chunks[-1][0]
    if tail < SPAN:
        fsend[len(chunks) - 1] = jnp.zeros(fsend.shape[1:], jnp.float32)
        gsend[len(chunks) - 1] = jnp.zeros(gsend.shape[1:], jnp.float32)

    lane1 = lax.broadcasted_iota(jnp.int32, (1, pix), 1)
    column = (me * RA_DEV + lane1 // NDEC).astype(jnp.float32)
    dec_row = (lane1 % NDEC).astype(jnp.float32)
    ra_turns = (column + 0.5) / (RA_DEV * n)
    sin_dec, cos_dec = sincos_turns(0.5 * ((dec_row + 0.5) / NDEC - 0.5))

    for cp in loads[:3]:
        cp.wait()
    lane = lax.broadcasted_iota(jnp.int32, (seg, pix), 1)
    for g in range(5):
        kept = jnp.zeros((seg, pix), jnp.float32)
        for j in range(RA_DEV):
            col = jnp.broadcast_to(
                sig_ref[:, g * RA_DEV + j : g * RA_DEV + j + 1].astype(jnp.float32), (seg, pix)
            )
            kept = jnp.where(lane // NDEC == j, col, kept)
        w = resp_ref[:, g * pix : (g + 1) * pix] * kept
        asend[g, 0:seg, :] = w
        asend[g, seg : 2 * seg, :] = w
        for s in range(2 * seg):
            asend[g, 2 * seg + s : 2 * seg + s + 1, :] = jnp.full((1, pix), sid_ref[s % seg])
    abuf[2] = asend[2]
    for cp in loads[3:6]:
        cp.wait()
    dh, dl = split(dir_ref[...])
    dcat = jnp.concatenate([dh, dh, dl], axis=1)
    residual = res_ref[...]
    rr = jnp.sum(residual * residual, axis=0, keepdims=True)

    pl.semaphore_wait(barrier, everyone - 1)

    def remote(src, dst, ss, rs, where):
        return pltpu.make_async_remote_copy(
            src_ref=src, dst_ref=dst, send_sem=ss, recv_sem=rs, device_id=where, device_id_type=MESH
        )

    a_copies = []
    for d in OFFSETS:
        g = d + 2
        cp = remote(asend.at[g], abuf.at[g], a_ss.at[g], a_rs.at[g], {"ra": ra_of(d)})
        cp.start()
        a_copies.append(cp)
    for cp in loads[6:]:
        cp.wait()
    noise = jnp.concatenate([noise_ref[...], noise_ref[...]], axis=0)
    b_copies = {}
    for batch, groups in enumerate(BATCHES):
        for g in groups:
            if g != 2:
                a_copies[OFFSETS.index(g - 2)].wait_recv()
        rows = len(groups) * 2 * seg
        weight = jnp.concatenate([abuf[g, 0 : 2 * seg, :] for g in groups], axis=0)
        sid = jnp.concatenate([abuf[g, 2 * seg : 4 * seg, :] for g in groups], axis=0)
        sin_h, cos_h = sincos_turns(ra_turns - sid * (1.0 / TWO_PI))
        delay = cos_dec * (baseline_x * cos_h + baseline_y * sin_h) + baseline_z * sin_dec
        row_id = lax.broadcasted_iota(jnp.int32, (rows, pix), 0)
        shift = jnp.where(lax.rem(row_id, 2 * seg) >= seg, 0.25, 0.0)
        half = bin_width * (SPAN - 1) / 2
        fine = [sincos_turns((half * float(nodes[r])) * delay) for r in range(count // 2)]
        for index, (k0, k1) in enumerate(chunks):
            centre = low_freq + bin_width * (
                (band * bins + k0).astype(jnp.float32) + (SPAN - 1) / 2
            )
            p = reduce_turns(centre * delay)
            t0 = weight * cos_turns(p - shift)
            t1 = weight * cos_turns(p - shift + 0.25)
            up, down = [], []
            for sin_d, cos_d in fine:
                a, b = t0 * cos_d, t1 * sin_d
                up.append(a + b)
                down.append(a - b)
            table = jnp.concatenate(up + down[::-1], axis=0)
            vh, vl = split(table)
            vh_refs[batch][index] = vh
            vl_refs[batch][index] = vl
            product = lax.dot_general(
                jnp.concatenate([vh, vl, vh], axis=1), dcat[k0:k1],
                (((1,), (1,)), ((), ())), preferred_element_type=jnp.float32,
            )
            total = lag_ref[0:1, 0 : k1 - k0] * product[0:rows]
            for r in range(1, count):
                total = total + (
                    lag_ref[r : r + 1, 0 : k1 - k0] * product[r * rows : (r + 1) * rows]
                )
            for at, g in enumerate(groups):
                fsend[index, g, :, 0 : k1 - k0] = total[at * 2 * seg : (at + 1) * 2 * seg]
                if g != 2:
                    cp = remote(
                        fsend.at[index, g], fbuf.at[index, g],
                        b_ss.at[index, g], b_rs.at[index, g], {"ra": ra_of(2 - g)},
                    )
                    cp.start()
                    b_copies[index, g] = cp

    c_copies = {}
    power = jnp.zeros((1, pix), jnp.float32)
    for index, (k0, k1) in enumerate(chunks):
        for d in OFFSETS:
            b_copies[index, d + 2].wait_recv()
        forward = fsend[index, 2, :, 0 : k1 - k0]
        for d in OFFSETS:
            forward = forward + fbuf[index, d + 2, :, 0 : k1 - k0]
        weighted = noise[:, k0:k1] * forward
        gsend[index, :, 0 : k1 - k0] = weighted
        for d in OFFSETS:
            g = d + 2
            cp = remote(
                gsend.at[index], gbuf.at[index, g],
                c_ss.at[index, g], c_rs.at[index, g], {"ra": ra_of(d)},
            )
            cp.start()
            c_copies[index, g] = cp
        gbuf[index, 2, :, 0 : k1 - k0] = weighted
        both = jnp.sum(weighted * forward, axis=0, keepdims=True)
        for q in range(0, k1 - k0, pix):
            piece = both[:, q : min(q + pix, k1 - k0)]
            if piece.shape[1] < pix:
                piece = jnp.concatenate(
                    [piece, jnp.zeros((1, pix - piece.shape[1]), jnp.float32)], axis=1
                )
            power = power + piece
    psend[0:1, 0:pix] = rr
    psend[0:1, pix : 2 * pix] = power

    def share(src, buf, ss, rs):
        each_peer(lambda i: remote(src, buf.at[i], ss.at[i], rs.at[i], peer(i)).start())

    def gathered(src, buf, ss, rs):
        each_peer(lambda i: remote(src, buf.at[i], ss.at[i], rs.at[i], peer(i)).wait_recv())
        return jnp.sum(buf[...], axis=0)

    def sent(src, buf, ss, rs):
        each_peer(lambda i: remote(src, buf.at[i], ss.at[i], rs.at[i], peer(i)).wait_send())

    pbuf[0] = psend[...]
    share(psend, pbuf, p_ss, p_rs)

    cross = jnp.zeros((1, pix), jnp.float32)
    norm = jnp.zeros((1, pix), jnp.float32)
    for batch, groups in enumerate(BATCHES):
        for index in range(len(chunks)):
            for j in groups:
                if j != 2:
                    c_copies[index, j].wait_recv()
        for index, (k0, k1) in enumerate(chunks):
            g = jnp.concatenate([gbuf[index, j, :, 0 : k1 - k0] for j in groups], axis=0)
            spread = jnp.concatenate(
                [lag_ref[r : r + 1, 0 : k1 - k0] * g for r in range(count)], axis=0
            )
            gh, gl = split(spread)
            vh, vl = vh_refs[batch][index], vl_refs[batch][index]
            image_t = lax.dot_general(
                jnp.concatenate([vh, vl, vh], axis=0), jnp.concatenate([gh, gh, gl], axis=0),
                (((0,), (0,)), ((), ())), preferred_element_type=jnp.float32,
            )
            if batch == 0:
                image_ref[k0:k1, :] = image_t.T
            else:
                image = image_ref[k0:k1, :] + image_t.T
                image_ref[k0:k1, :] = image
                cross = cross + jnp.sum(image * res_ref[k0:k1, :], axis=0, keepdims=True)
                norm = norm + jnp.sum(image * image, axis=0, keepdims=True)

    esend[0:1, 0:pix] = cross
    esend[0:1, pix : 2 * pix] = norm
    ebuf[0] = esend[...]
    share(esend, ebuf, e_ss, e_rs)
    totals = gathered(psend, pbuf, p_ss, p_rs)
    rr_all = jnp.sum(totals[:, 0:pix], axis=1, keepdims=True)
    power_all = jnp.sum(totals[:, pix : 2 * pix], axis=1, keepdims=True)
    alpha = (rr_all + epsilon) / (power_all + epsilon)
    sol_out[...] = est_ref[...] + alpha * dir_ref[...]
    res_out[...] = res_ref[...] - alpha * image_ref[...]
    for cp in a_copies + list(b_copies.values()) + list(c_copies.values()):
        cp.wait_send()
    sent(psend, pbuf, p_ss, p_rs)
    totals = gathered(esend, ebuf, e_ss, e_rs)
    cross_all = jnp.sum(totals[:, 0:pix], axis=1, keepdims=True)
    norm_all = jnp.sum(totals[:, pix : 2 * pix], axis=1, keepdims=True)
    norm_next = rr_all - 2.0 * alpha * cross_all + alpha * alpha * norm_all
    beta = norm_next / (rr_all + epsilon)
    dir_out[...] = res_out[...] + beta * dir_ref[...]
    sent(esend, ebuf, e_ss, e_rs)


def solution(mesh):
    n, m = mesh.shape["ra"], mesh.shape["freq"]

    def shards(estimate, residual, direction, sidereal, response, significant, inv_noise):
        bins, pix = direction.shape
        seg = sidereal.shape[0]
        count = node_count()
        nodes, lagrange = lagrange_rows(count)
        pieces = -(-bins // SPAN)
        f32, bf16 = jnp.float32, jnp.bfloat16
        vmem = pl.BlockSpec(memory_space=pltpu.VMEM)
        dma = pltpu.SemaphoreType.DMA
        operands = (
            sidereal, response, significant, inv_noise, jnp.asarray(lagrange),
            direction, residual, estimate,
        )
        updated = pl.pallas_call(
            functools.partial(kernel, n, m, nodes),
            out_shape=(pltpu.VMEM((bins, pix), f32),) * 3,
            in_specs=[pl.BlockSpec(memory_space=pl.ANY)] * len(operands),
            out_specs=(vmem,) * 3,
            scratch_shapes=[pltpu.SMEM(sidereal.shape, f32)]
            + [pltpu.VMEM(x.shape, x.dtype) for x in operands[1:]]
            + [
                pltpu.VMEM((5, 4 * seg, pix), f32),
                pltpu.VMEM((5, 4 * seg, pix), f32),
                pltpu.VMEM((pieces, 5, 2 * seg, SPAN), f32),
                pltpu.VMEM((pieces, 5, 2 * seg, SPAN), f32),
                pltpu.VMEM((pieces, 2 * seg, SPAN), f32),
                pltpu.VMEM((pieces, 5, 2 * seg, SPAN), f32),
                [pltpu.VMEM((pieces, count * 2 * seg * len(b), pix), bf16) for b in BATCHES],
                [pltpu.VMEM((pieces, count * 2 * seg * len(b), pix), bf16) for b in BATCHES],
                pltpu.VMEM((bins, pix), f32),
                pltpu.VMEM((1, 2 * pix), f32),
                pltpu.VMEM((n * m, 1, 2 * pix), f32),
                pltpu.VMEM((1, 2 * pix), f32),
                pltpu.VMEM((n * m, 1, 2 * pix), f32),
                dma((len(operands),)),
            ]
            + [dma((5,))] * 2
            + [dma((pieces, 5))] * 4
            + [dma((n * m,))] * 4,
            compiler_params=pltpu.CompilerParams(collective_id=0, has_side_effects=True),
        )(*operands)
        return updated

    return jax.shard_map(
        shards,
        mesh=mesh,
        in_specs=(
            P("freq", "ra"),
            P("freq", "ra"),
            P("freq", "ra"),
            P("ra"),
            P("ra", None),
            P("ra", None),
            P("ra", "freq"),
        ),
        out_specs=(P("freq", "ra"), P("freq", "ra"), P("freq", "ra")),
        check_vma=False,
    )
```
